256 devices in a mesh: gx: 32 (over x, y, core), gy: 8 (over z).
Axes of the slice: x: 4, y: 4, z: 8, core: 2. Of those that a mesh axis runs over, the one named last changes fastest.
Arguments:
- right_side: float32 [64, 32768], P(None, ('gx', 'gy')), may hold values from -14 to 14
- pressure_head: float32 [64, 32768], P(None, ('gx', 'gy')), may hold values from -3 to -0.1
- vg_alpha: float32 [32768], P(('gx', 'gy')), may hold values from 0.5 to 5
- live_counts: int32 [256], P(('gx', 'gy')), may hold values from 16 to 128, as said below
- partners: int32 [4, 32768], P(None, ('gx', 'gy')), may hold values from 0 to 127, as said below
- element_blocks: bfloat16 [64, 64, 32768], P(None, None, ('gx', 'gy')), may hold values from -1.5 to 9
- face_blocks: bfloat16 [4, 64, 64, 32768], P(None, None, None, ('gx', 'gy')), may hold values from -1 to 1
- local_inverse: bfloat16 [64, 64, 32768], P(None, None, ('gx', 'gy')), may hold values from -0.11 to 0.27
- coarse_basis: bfloat16 [64, 64, 32768], P(None, None, ('gx', 'gy')), may hold values from -0.125 to 0.125
- coarse_inverse: bfloat16 [16384, 16384], P(('gx', 'gy')), may hold values from -1 to 1, as said below
Outputs:
- update: float32 [64, 32768], P(None, ('gx', 'gy'))
- hessenberg: float32 [3, 2], replicated
The draws below stay inside these ranges and needn't reach their ends.
Inputs may be any that keep to these rules, and one draw needn't show every extreme that they name: `live_counts`: some subdomain has all 128 slots live. `partners`: each partner is a live slot of the neighbouring subdomain when that subdomain exists. coarse_inverse is symmetric.
All inputs are finite; a program needn't handle non-finite values.
Results may differ from the reference program's by a relative error of at most 0.0003.
Values sent between devices are 32-bit elements; how exact they have to be, the bound alone decides.
No kernel may reach another device: no remote copies, remote signals or barrier semaphores. Data moves between devices by JAX's collectives and lax.ppermute only.
A program may use at most 128 MiB of HBM per device.

```python
import math
import jax
import jax.numpy as jnp
from jax import lax

NODES = 64
MODES = 64
E_DEV = 128
NE = 32768
NC = 16384
N_GX = 32
N_GY = 8


def count_table(key):
    subdomains = N_GX * N_GY
    lowest = max(1, E_DEV // 8)
    baseline = jax.random.randint(jax.random.fold_in(key, 11), (subdomains,), lowest, E_DEV // 4 + 2)
    full_pick = jax.random.randint(jax.random.fold_in(key, 12), (subdomains,), 0, 8) == 0
    forced = jnp.arange(subdomains) == jax.random.randint(jax.random.fold_in(key, 13), (), 0, subdomains)
    return jnp.where(full_pick | forced, E_DEV, baseline).astype(jnp.int32)


def draw_live_counts(key, part):
    return count_table(key)


def draw_partners(key, part):
    table = count_table(key).reshape(N_GX, N_GY)
    beside = jnp.stack([jnp.roll(table, 1, 0), jnp.roll(table, -1, 0), jnp.roll(table, 1, 1), jnp.roll(table, -1, 1)])
    limits = jnp.broadcast_to(beside[:, :, :, None], (4, N_GX, N_GY, E_DEV))
    picked = jax.random.randint(jax.random.fold_in(key, 21), (4, N_GX, N_GY, E_DEV), 0, limits)
    return picked.reshape(4, NE).astype(jnp.int32)


def draw_right_side(key, part):
    column_scale = jnp.exp(1.2 * jax.random.uniform(jax.random.fold_in(key, 31), (1, NE), jnp.float32, -1.0, 1.0))
    values = jnp.clip(jax.random.normal(jax.random.fold_in(key, 33), (NODES, NE), jnp.float32), -4.0, 4.0)
    return values * column_scale


def diagonal_mask():
    return jnp.arange(NODES)[:, None, None] == jnp.arange(NODES)[None, :, None]


def draw_element_blocks(key, part):
    diagonal = jax.random.uniform(jax.random.fold_in(key, 43), (NODES, NODES, NE), jnp.float32, 4.0, 8.0)
    offdiag = jnp.clip(0.25 * jax.random.normal(jax.random.fold_in(key, 44), (NODES, NODES, NE), jnp.float32), -1.5, 1.5)
    return jnp.where(diagonal_mask(), diagonal, offdiag).astype(jnp.bfloat16)


def draw_local_inverse(key, part):
    diagonal = jax.random.uniform(jax.random.fold_in(key, 53), (NODES, NODES, NE), jnp.float32, 0.125, 0.25)
    offdiag = jnp.clip(0.02 * jax.random.normal(jax.random.fold_in(key, 54), (NODES, NODES, NE), jnp.float32), -0.1, 0.1)
    return jnp.where(diagonal_mask(), diagonal, offdiag).astype(jnp.bfloat16)


def draw_coarse_inverse(key, part):
    noise = jnp.clip(jax.random.normal(jax.random.fold_in(key, 62), (NC, NC), jnp.float32), -5.0, 5.0)
    offdiag = (noise + noise.T) * (0.35 / math.sqrt(NC))
    diagonal = jax.random.uniform(jax.random.fold_in(key, 63), (NC,), jnp.float32, 0.5, 1.0)
    same = jnp.arange(NC)[:, None] == jnp.arange(NC)[None, :]
    return jnp.where(same, diagonal[:, None], jnp.clip(offdiag, -1.0, 1.0)).astype(jnp.bfloat16)


def level_of(stream_key, extent, cuts, smallest, high):
    def one(dim, shards_of):
        steps = jax.random.uniform(jax.random.fold_in(jax.random.fold_in(stream_key, 6), dim), (shards_of,), jnp.float32, smallest / len(cuts), high / len(cuts))
        return jnp.repeat(jnp.exp(steps), extent[dim] // shards_of).reshape((-1,) + (1,) * (len(extent) - dim - 1))

    gain = one(*cuts[0])
    for cut in cuts[1:]:
        gain = gain * one(*cut)
    return gain


def gaussian(key, extent, width, bound, shards=(), held_as=jnp.bfloat16):
    drawn = width * jax.random.normal(key, extent, jnp.float32)
    if shards:
        drawn = drawn * level_of(key, extent, shards, -0.22, 0.18)
    return jnp.clip(drawn, -bound, bound).astype(held_as)


def setup_inputs(seed: int = 0) -> dict:
    key_list = jax.random.split(jax.random.key(seed), 11)
    right_side = draw_right_side(jax.random.fold_in(key_list[10], 71), 0)
    pressure_head = jnp.clip(-3.0 + 2.9 * jax.random.uniform(key_list[1], (NODES, NE), jnp.float32) ** level_of(key_list[1], (NODES, NE), ((1, 256),), -0.2, 0.2), -3.0, -0.1)
    vg_alpha = jnp.clip(jnp.exp(math.log(5.0) - 2.3025851 * jax.random.uniform(key_list[2], (NE,), jnp.float32) ** level_of(key_list[2], (NE,), ((0, 256),), -0.2, 0.2)), 0.5, 5.0)
    live_counts = draw_live_counts(jax.random.fold_in(key_list[10], 71), 0)
    partners = draw_partners(jax.random.fold_in(key_list[10], 71), 0)
    element_blocks = draw_element_blocks(jax.random.fold_in(key_list[10], 71), 0)
    face_blocks = gaussian(key_list[6], (4, NODES, NODES, NE), (NODES // 2) ** -0.5, 1.0, ((3, 256),))
    local_inverse = draw_local_inverse(jax.random.fold_in(key_list[10], 71), 0)
    coarse_basis = gaussian(key_list[8], (MODES, NODES, NE), (NODES * E_DEV // 4) ** -0.5, 0.125, ((2, 256),))
    coarse_inverse = draw_coarse_inverse(jax.random.fold_in(key_list[10], 71), 0)
    return {"right_side": right_side, "pressure_head": pressure_head, "vg_alpha": vg_alpha, "live_counts": live_counts, "partners": partners, "element_blocks": element_blocks, "face_blocks": face_blocks, "local_inverse": local_inverse, "coarse_basis": coarse_basis, "coarse_inverse": coarse_inverse}


highest = lax.Precision.HIGHEST
shape_exponent = 1.6
time_factor = 4.0

def capacity(pressure, alpha_row):
    scaled = jnp.abs(alpha_row[None, :] * pressure)
    expo_m = 1.0 - 1.0 / shape_exponent
    return time_factor * alpha_row[None, :] * shape_exponent * expo_m * jnp.power(scaled, shape_exponent - 1.0) * jnp.power(1.0 + jnp.power(scaled, shape_exponent), -(expo_m + 1.0))

def apply_blocks(blocks, vector_in):
    return jnp.einsum('ije,je->ie', blocks.astype(jnp.float32), vector_in, precision=highest)

def reference(right_side, pressure_head, vg_alpha, live_counts, partners, element_blocks, face_blocks, local_inverse, coarse_basis, coarse_inverse):
    subdomains = N_GX * N_GY
    slot_ids = jnp.arange(E_DEV, dtype=jnp.int32)
    live_mask = (slot_ids[None, :] < live_counts[:, None]).astype(jnp.float32).reshape(1, NE)
    storage = capacity(pressure_head, vg_alpha)

    def neighbour_values(vector_in):
        layout = vector_in.reshape(NODES, N_GX, N_GY, E_DEV)
        edge_x = jnp.zeros((NODES, 1, N_GY, E_DEV), jnp.float32)
        edge_y = jnp.zeros((NODES, N_GX, 1, E_DEV), jnp.float32)
        from_west = jnp.concatenate([edge_x, layout[:, :-1]], axis=1)
        from_east = jnp.concatenate([layout[:, 1:], edge_x], axis=1)
        from_south = jnp.concatenate([edge_y, layout[:, :, :-1]], axis=2)
        from_north = jnp.concatenate([layout[:, :, 1:], edge_y], axis=2)
        return (from_west, from_east, from_south, from_north)

    def operate(vector_in):
        summed = apply_blocks(element_blocks, vector_in) + storage * vector_in
        for direction, source in enumerate(neighbour_values(vector_in)):
            gather_ids = jnp.broadcast_to(partners[direction].astype(jnp.int32).reshape(1, N_GX, N_GY, E_DEV), source.shape)
            picked = jnp.take_along_axis(source, gather_ids, axis=3).reshape(NODES, NE)
            summed = summed + apply_blocks(face_blocks[direction], picked)
        return summed * live_mask

    def precondition(vector_in):
        local_part = apply_blocks(local_inverse, vector_in)
        basis_grid = coarse_basis.astype(jnp.float32).reshape(MODES, NODES, subdomains, E_DEV)
        restricted = jnp.einsum('mjde,jde->dm', basis_grid, vector_in.reshape(NODES, subdomains, E_DEV), precision=highest).reshape(NC)
        row_blocks = coarse_inverse.reshape(subdomains, MODES, NC)
        coarse_part = lax.map(lambda coarse_rows: jnp.dot(coarse_rows.astype(jnp.float32), restricted, precision=highest), row_blocks)
        prolonged = jnp.einsum('mjde,dm->jde', basis_grid, coarse_part, precision=highest).reshape(NODES, NE)
        return (local_part + prolonged) * live_mask
    rhs_live = right_side * live_mask
    start_size = jnp.sqrt(jnp.sum(rhs_live * rhs_live))
    krylov = [rhs_live / start_size]
    directions = []
    columns = []
    for sweep in range(2):
        prepared = precondition(krylov[-1])
        directions.append(prepared)
        mapped = operate(prepared)
        coeffs = jnp.stack([jnp.sum(mapped * member) for member in krylov])
        remains = mapped
        for position, member in enumerate(krylov):
            remains = remains - coeffs[position] * member
        height = jnp.sqrt(jnp.sum(remains * remains))
        columns.append((coeffs, height))
        if sweep == 0:
            krylov.append(remains / height)
    h_one_one = columns[0][0][0]
    h_two_one = columns[0][1]
    h_one_two = columns[1][0][0]
    h_two_two = columns[1][0][1]
    h_three_two = columns[1][1]
    zero_entry = jnp.zeros((), jnp.float32)
    hessenberg = jnp.stack([jnp.stack([h_one_one, h_one_two]), jnp.stack([h_two_one, h_two_two]), jnp.stack([zero_entry, h_three_two])])
    gram_aa = h_one_one * h_one_one + h_two_one * h_two_one
    gram_ab = h_one_one * h_one_two + h_two_one * h_two_two
    gram_bb = h_one_two * h_one_two + h_two_two * h_two_two + h_three_two * h_three_two
    target_a = start_size * h_one_one
    target_b = start_size * h_one_two
    determinant = gram_aa * gram_bb - gram_ab * gram_ab
    weight_one = (gram_bb * target_a - gram_ab * target_b) / determinant
    weight_two = (gram_aa * target_b - gram_ab * target_a) / determinant
    update = weight_one * directions[0] + weight_two * directions[1]
    return (update, hessenberg)
```

```python
import jax
import jax.numpy as jnp
from jax import lax
from jax.experimental import pallas as pl
from jax.experimental.pallas import tpu as pltpu
from jax.sharding import PartitionSpec as P

shape_exponent = 1.6
time_factor = 4.0
expo_m = 1.0 - 1.0 / shape_exponent

NODES = 64
MODES = 64
SLOTS = 128
DOTS = 8
ROWS = MODES + DOTS
F32 = jnp.float32
VM = pl.BlockSpec(memory_space=pltpu.VMEM)
SM = pl.BlockSpec(memory_space=pltpu.SMEM)


def live_mask(count):
    slots = lax.broadcasted_iota(jnp.int32, (1, SLOTS), 1)
    return (slots < count).astype(F32)


def tile_sum(block):
    parts = [block[8 * t : 8 * t + 8] for t in range(8)]
    while len(parts) > 1:
        parts = [a + b for a, b in zip(parts[::2], parts[1::2])]
    return parts[0]


def fold_rows(partial_ref, rows):
    parts = [partial_ref[pl.ds(k, rows, stride=8), :] for k in range(8)]
    while len(parts) > 1:
        parts = [a + b for a, b in zip(parts[::2], parts[1::2])]
    return parts[0]


def blocks_into(partial_ref, terms):
    def body(i, carry):
        total = None
        for block_at, vector in terms:
            part = tile_sum(block_at(i).astype(F32) * vector())
            total = part if total is None else total + part
        partial_ref[pl.ds(pl.multiple_of(8 * i, 8), 8), :] = total
        return carry

    lax.fori_loop(0, NODES, body, 0, unroll=4)


def send_row(partial_ref, out_ref):
    square = jnp.concatenate(
        [fold_rows(partial_ref, ROWS), jnp.zeros((SLOTS - ROWS, SLOTS), F32)], axis=0
    )
    row = jnp.sum(square.T, axis=0, keepdims=True)
    out_ref[...] = jnp.broadcast_to(row, out_ref.shape)


def put_dots(partial_ref, pairs):
    for k in range(DOTS):
        rows = pl.ds(8 * (MODES + k), 8)
        if k < len(pairs):
            left, right = pairs[k]
            partial_ref[rows, :] = tile_sum(left * right)
        else:
            partial_ref[rows, :] = jnp.zeros((8, SLOTS), F32)


def restrict_kernel(count_ref, rhs_ref, basis_ref, row_ref, partial_ref):
    b = rhs_ref[...] * live_mask(count_ref[0])
    blocks_into(partial_ref, [(lambda m: basis_ref[m], lambda: b)])
    put_dots(partial_ref, [])
    send_row(partial_ref, row_ref)


def halves(rows_ref):
    lane = lax.broadcasted_iota(jnp.int32, (SLOTS, SLOTS), 1)
    even = rows_ref[pl.ds(0, SLOTS, stride=2), :]
    odd = rows_ref[pl.ds(1, SLOTS, stride=2), :]
    return jnp.where(lane < MODES, even, pltpu.roll(odd, MODES, 1))


def precondition(v_ref, coarse_ref, inverse_ref, local_ref, basis_ref, partial_ref, modal_ref):
    def coarse_step(t, acc):
        column = inverse_ref[:, pl.ds(pl.multiple_of(t * SLOTS, SLOTS), SLOTS)].astype(F32)
        return acc + column * coarse_ref[pl.ds(t, 1), :]

    acc = lax.fori_loop(0, 2 * MODES, coarse_step, jnp.zeros((MODES, SLOTS), F32), unroll=8)
    modal_ref[...] = jnp.broadcast_to(jnp.sum(acc, axis=1, keepdims=True), (MODES, SLOTS))
    blocks_into(partial_ref, [(lambda i: local_ref[i], lambda: v_ref[...])])

    def prolong_step(m, total):
        return total + basis_ref[m].astype(F32) * modal_ref[pl.ds(m, 1), :]

    total = lax.fori_loop(0, MODES, prolong_step, jnp.zeros((NODES, SLOTS), F32), unroll=8)
    return total + fold_rows(partial_ref, NODES)


def first_kernel(
    count_ref, rhs_ref, gathered_ref, inverse_ref, local_ref, basis_ref,
    z_ref, coarse_ref, b_ref, partial_ref, modal_ref,
):
    mask = live_mask(count_ref[0])
    coarse_ref[...] = halves(gathered_ref)
    b_ref[...] = rhs_ref[...] * mask
    z = precondition(b_ref, coarse_ref, inverse_ref, local_ref, basis_ref, partial_ref, modal_ref)
    z_ref[...] = z * mask


def lane_of(row, k):
    lane = lax.broadcasted_iota(jnp.int32, row.shape, 1)
    return jnp.sum(jnp.where(lane == k, row, 0.0), axis=1, keepdims=True)


def second_kernel(
    b_ref, w_ref, count_ref, coarse_ref, gathered_ref, inverse_ref, local_ref, basis_ref,
    z_ref, v_ref, sums_ref, mixed_ref, partial_ref, modal_ref,
):
    mask = live_mask(count_ref[0])
    sums = jnp.sum(gathered_ref[...], axis=0, keepdims=True)
    sums_ref[...] = jnp.broadcast_to(sums, sums_ref.shape)
    along = lane_of(sums, MODES) / lane_of(sums, MODES + 2)
    scale = 1.0 / jnp.sqrt(lane_of(sums, MODES + 1))
    mixed_ref[...] = (halves(gathered_ref) - along * coarse_ref[...]) * scale
    v_ref[...] = (w_ref[...] - along * b_ref[...]) * scale
    z = precondition(v_ref, mixed_ref, inverse_ref, local_ref, basis_ref, partial_ref, modal_ref)
    z_ref[...] = z * mask


def own_kernel(z_ref, blocks_ref, pressure_ref, alpha_ref, out_ref, partial_ref):
    blocks_into(partial_ref, [(lambda i: blocks_ref[i], lambda: z_ref[...])])
    alpha = alpha_ref[...]
    scaled = jnp.abs(alpha * pressure_ref[...])
    power = jnp.exp((shape_exponent - 1.0) * jnp.log(scaled))
    tail = jnp.exp(-(expo_m + 1.0) * jnp.log(1.0 + power * scaled))
    storage = (time_factor * shape_exponent * expo_m) * alpha * power * tail
    out_ref[...] = fold_rows(partial_ref, NODES) + storage * z_ref[...]


def faces_sum(own_ref, count_ref, faces_ref, partners_ref, source_refs, blocks_ref, picked_ref, partial_ref):
    for q, source_ref in enumerate(source_refs):
        slots = jnp.broadcast_to(partners_ref[pl.ds(faces_ref[q], 1), :], (NODES, SLOTS))
        picked_ref[q] = jnp.take_along_axis(source_ref[...], slots, axis=1)
    faces = [faces_ref[q] for q in range(4)]
    blocks_into(
        partial_ref,
        [(lambda i, q=q: blocks_ref[faces[q], i], lambda q=q: picked_ref[q]) for q in range(4)],
    )
    return (own_ref[...] + fold_rows(partial_ref, NODES)) * live_mask(count_ref[0])


def image_kernel(
    own_ref, count_ref, faces_ref, partners_ref, s0, s1, s2, s3, blocks_ref, b_ref, basis_ref,
    w_ref, row_ref, picked_ref, partial_ref,
):
    w_ref[...] = faces_sum(
        own_ref, count_ref, faces_ref, partners_ref, (s0, s1, s2, s3), blocks_ref, picked_ref, partial_ref
    )
    blocks_into(partial_ref, [(lambda m: basis_ref[m], lambda: w_ref[...])])
    w = w_ref[...]
    b = b_ref[...]
    put_dots(partial_ref, [(w, b), (w, w), (b, b)])
    send_row(partial_ref, row_ref)


def last_image_kernel(
    own_ref, count_ref, faces_ref, partners_ref, s0, s1, s2, s3, blocks_ref, b_ref, v_ref,
    row_ref, picked_ref, partial_ref,
):
    w = faces_sum(
        own_ref, count_ref, faces_ref, partners_ref, (s0, s1, s2, s3), blocks_ref, picked_ref, partial_ref
    )
    b = b_ref[...]
    v = v_ref[...]
    partial_ref[pl.ds(0, 8 * MODES), :] = jnp.zeros((8 * MODES, SLOTS), F32)
    put_dots(partial_ref, [(w, b), (w, v), (w, w), (v, v), (b, v)])
    send_row(partial_ref, row_ref)


def final_kernel(first_ref, gathered_ref, z1_ref, z2_ref, update_ref, hess_ref):
    sums = first_ref[0:1, :]
    late = jnp.sum(gathered_ref[...], axis=0, keepdims=True)
    wb, ww, bb = (lane_of(sums, MODES + k) for k in range(3))
    xb, xv, xx, vv, bv = (lane_of(late, MODES + k) for k in range(5))
    beta = jnp.sqrt(bb)
    size = jnp.sqrt(vv)
    h11 = wb / bb
    h21 = size * jnp.sqrt(ww) / beta
    h12 = xb / (size * beta)
    h22 = xv / vv
    cross = bv / (beta * size)
    rest = xx / vv - h12 * h12 - h22 * h22 + 2.0 * h12 * h22 * cross
    h32 = jnp.sqrt(jnp.maximum(rest, 0.0))
    gram_aa = h11 * h11 + h21 * h21
    gram_ab = h11 * h12 + h21 * h22
    gram_bb = h12 * h12 + h22 * h22 + h32 * h32
    target_a = beta * h11
    target_b = beta * h12
    determinant = gram_aa * gram_bb - gram_ab * gram_ab
    weight_one = (gram_bb * target_a - gram_ab * target_b) / determinant
    weight_two = (gram_aa * target_b - gram_ab * target_a) / determinant
    update_ref[...] = (weight_one / beta) * z1_ref[...] + (weight_two / size) * z2_ref[...]
    row = lax.broadcasted_iota(jnp.int32, (2, 3), 0)
    col = lax.broadcasted_iota(jnp.int32, (2, 3), 1)
    hess = jnp.where(row == 0, jnp.where(col == 0, h11, h21), jnp.where(col == 0, h12, jnp.where(col == 1, h22, h32)))
    hess_ref[...] = jnp.where((row == 0) & (col == 2), 0.0, hess)


def vec(*shape):
    return jax.ShapeDtypeStruct(shape, F32)


def call(body, name, specs, outs, scratch, megabytes=4):
    return pl.pallas_call(
        body,
        name=name,
        in_specs=specs,
        out_specs=jax.tree.map(lambda _: VM, outs),
        out_shape=outs,
        scratch_shapes=scratch,
        compiler_params=pltpu.CompilerParams(vmem_limit_bytes=megabytes << 20),
    )


def swaps(mesh_shape):
    n_gx, n_gy = mesh_shape
    at = lambda i, j: i * n_gy + j
    pairs = ([], [], [], [])
    for i in range(n_gx):
        for j in range(n_gy):
            if i + 1 < n_gx:
                pairs[i % 2] .extend([(at(i, j), at(i + 1, j)), (at(i + 1, j), at(i, j))])
            if j + 1 < n_gy:
                pairs[2 + j % 2].extend([(at(i, j), at(i, j + 1)), (at(i, j + 1), at(i, j))])
    return pairs


def solution(mesh):
    axes = ("gx", "gy")
    n_gx, n_gy = mesh.shape["gx"], mesh.shape["gy"]
    total = n_gx * n_gy
    pairs = swaps((n_gx, n_gy))

    def exchange(rows):
        return lax.all_to_all(rows, axes, 0, 0, tiled=True)

    def shards(
        right_side, pressure_head, vg_alpha, live_counts, partners,
        element_blocks, face_blocks, local_inverse, coarse_basis, coarse_inverse,
    ):
        alpha = vg_alpha.reshape(1, SLOTS)
        odd_x = lax.rem(lax.axis_index("gx"), 2)
        odd_y = lax.rem(lax.axis_index("gy"), 2)
        faces = jnp.stack([1 - odd_x, odd_x, 3 - odd_y, 2 + odd_y]).astype(jnp.int32)
        partial = pltpu.VMEM((8 * ROWS, SLOTS), F32)
        picked = pltpu.VMEM((4, NODES, SLOTS), F32)
        modal = pltpu.VMEM((MODES, SLOTS), F32)

        rows = call(restrict_kernel, "restrict", [SM, VM, VM], vec(total, SLOTS), [partial])(
            live_counts, right_side, coarse_basis
        )
        gathered = exchange(rows)
        z1, coarse, b = call(
            first_kernel, "first", [SM] + [VM] * 5,
            (vec(NODES, SLOTS), vec(SLOTS, SLOTS), vec(NODES, SLOTS)), [partial, modal],
        )(live_counts, right_side, gathered, coarse_inverse, local_inverse, coarse_basis)

        def neighbours(z):
            return [lax.ppermute(z, axes, p) for p in pairs]

        def own(z):
            return call(own_kernel, "own", [VM] * 4, vec(NODES, SLOTS), [partial])(
                z, element_blocks, pressure_head, alpha
            )

        sources = neighbours(z1)
        w1, rows = call(
            image_kernel, "image", [VM, SM, SM] + [VM] * 8,
            (vec(NODES, SLOTS), vec(total, SLOTS)), [picked, partial],
        )(own(z1), live_counts, faces, partners, *sources, face_blocks, b, coarse_basis)
        gathered = exchange(rows)
        z2, v2, sums = call(
            second_kernel, "second", [VM, VM, SM] + [VM] * 5,
            (vec(NODES, SLOTS), vec(NODES, SLOTS), vec(8, SLOTS)),
            [pltpu.VMEM((SLOTS, SLOTS), F32), partial, modal],
        )(b, w1, live_counts, coarse, gathered, coarse_inverse, local_inverse, coarse_basis)
        sources = neighbours(z2)
        rows = call(
            last_image_kernel, "last_image", [VM, SM, SM] + [VM] * 8,
            vec(total, SLOTS), [picked, partial],
        )(own(z2), live_counts, faces, partners, *sources, face_blocks, b, v2)
        gathered = exchange(rows)
        update, hess = call(
            final_kernel, "final", [VM] * 4, (vec(NODES, SLOTS), vec(2, 3)), []
        )(sums, gathered, z1, z2)
        return update, hess.T

    placed = (
        P(None, axes), P(None, axes), P(axes), P(axes), P(None, axes),
        P(None, None, axes), P(None, None, None, axes), P(None, None, axes), P(None, None, axes),
        P(axes, None),
    )
    return jax.shard_map(
        shards, mesh=mesh, in_specs=placed, out_specs=(P(None, axes), P()), check_vma=False
    )
```

```python
import jax
import jax.numpy as jnp
from jax import lax
from jax.experimental import pallas as pl
from jax.experimental.pallas import tpu as pltpu
from jax.sharding import PartitionSpec as P

shape_exponent = 1.6
time_factor = 4.0
expo_m = 1.0 - 1.0 / shape_exponent

NODES = 64
MODES = 64
SLOTS = 128
DOTS = 8
ROWS = MODES + DOTS
F32 = jnp.float32
VM = pl.BlockSpec(memory_space=pltpu.VMEM)
SM = pl.BlockSpec(memory_space=pltpu.SMEM)
HB = pl.BlockSpec(memory_space=pltpu.HBM)
PIECES = 4
ORDER = (0, 2, 3, 1)


def live_mask(count):
    slots = lax.broadcasted_iota(jnp.int32, (1, SLOTS), 1)
    return (slots < count).astype(F32)


def tile_sum(block):
    parts = [block[8 * t : 8 * t + 8] for t in range(8)]
    while len(parts) > 1:
        parts = [a + b for a, b in zip(parts[::2], parts[1::2])]
    return parts[0]


def fold_rows(partial_ref, rows):
    parts = [partial_ref[pl.ds(k, rows, stride=8), :] for k in range(8)]
    while len(parts) > 1:
        parts = [a + b for a, b in zip(parts[::2], parts[1::2])]
    return parts[0]


def blocks_into(partial_ref, terms, first=0, last=NODES):
    def body(i, carry):
        total = None
        for block_at, vector in terms:
            part = tile_sum(block_at(i).astype(F32) * vector())
            total = part if total is None else total + part
        partial_ref[pl.ds(pl.multiple_of(8 * i, 8), 8), :] = total
        return carry

    lax.fori_loop(first, last, body, 0, unroll=4)


def send_row(partial_ref, out_ref):
    square = jnp.concatenate(
        [fold_rows(partial_ref, ROWS), jnp.zeros((SLOTS - ROWS, SLOTS), F32)], axis=0
    )
    row = jnp.sum(square.T, axis=0, keepdims=True)
    out_ref[...] = jnp.broadcast_to(row, out_ref.shape)


def put_dots(partial_ref, pairs):
    for k in range(DOTS):
        rows = pl.ds(8 * (MODES + k), 8)
        if k < len(pairs):
            left, right = pairs[k]
            partial_ref[rows, :] = tile_sum(left * right)
        else:
            partial_ref[rows, :] = jnp.zeros((8, SLOTS), F32)


def restrict_kernel(
    count_ref, rhs_hbm, basis_hbm, local_hbm, inverse_hbm,
    row_ref, b_ref, basis_ref, local_ref, inverse_ref,
    partial_ref, rhs_sem, basis_sem, local_sem, inverse_sem,
):
    rhs_copy = pltpu.make_async_copy(rhs_hbm, b_ref, rhs_sem)
    rhs_copy.start()
    modes = MODES // PIECES
    copies = []
    for k in range(PIECES):
        piece = pl.ds(k * modes, modes)
        copies.append(pltpu.make_async_copy(basis_hbm.at[piece], basis_ref.at[piece], basis_sem.at[k]))
        copies[-1].start()
    local_copy = pltpu.make_async_copy(local_hbm, local_ref, local_sem)
    local_copy.start()
    inverse_copy = pltpu.make_async_copy(inverse_hbm, inverse_ref, inverse_sem)
    inverse_copy.start()
    put_dots(partial_ref, [])
    rhs_copy.wait()
    b_ref[...] = b_ref[...] * live_mask(count_ref[0])
    for k, copy in enumerate(copies):
        copy.wait()
        blocks_into(
            partial_ref, [(lambda m: basis_ref[m], lambda: b_ref[...])], k * modes, (k + 1) * modes
        )
    send_row(partial_ref, row_ref)
    local_copy.wait()
    inverse_copy.wait()


def halves(rows_ref):
    lane = lax.broadcasted_iota(jnp.int32, (SLOTS, SLOTS), 1)
    even = rows_ref[pl.ds(0, SLOTS, stride=2), :]
    odd = rows_ref[pl.ds(1, SLOTS, stride=2), :]
    return jnp.where(lane < MODES, even, pltpu.roll(odd, MODES, 1))


def precondition(v_ref, coarse_ref, inverse_ref, local_ref, basis_ref, partial_ref, modal_ref):
    def coarse_step(t, acc):
        column = inverse_ref[:, pl.ds(pl.multiple_of(t * SLOTS, SLOTS), SLOTS)].astype(F32)
        return acc + column * coarse_ref[pl.ds(t, 1), :]

    acc = lax.fori_loop(0, 2 * MODES, coarse_step, jnp.zeros((MODES, SLOTS), F32), unroll=8)
    modal_ref[...] = jnp.broadcast_to(jnp.sum(acc, axis=1, keepdims=True), (MODES, SLOTS))
    blocks_into(partial_ref, [(lambda i: local_ref[i], lambda: v_ref[...])])

    def prolong_step(m, total):
        return total + basis_ref[m].astype(F32) * modal_ref[pl.ds(m, 1), :]

    total = lax.fori_loop(0, MODES, prolong_step, jnp.zeros((NODES, SLOTS), F32), unroll=8)
    return total + fold_rows(partial_ref, NODES)


def first_kernel(
    count_ref, b_ref, gathered_ref, inverse_ref, local_ref, basis_ref,
    z_ref, coarse_ref, partial_ref, modal_ref,
):
    mask = live_mask(count_ref[0])
    coarse_ref[...] = halves(gathered_ref)
    z = precondition(b_ref, coarse_ref, inverse_ref, local_ref, basis_ref, partial_ref, modal_ref)
    z_ref[...] = z * mask


def lane_of(row, k):
    lane = lax.broadcasted_iota(jnp.int32, row.shape, 1)
    return jnp.sum(jnp.where(lane == k, row, 0.0), axis=1, keepdims=True)


def second_kernel(
    b_ref, w_ref, count_ref, coarse_ref, gathered_ref, inverse_ref, local_ref, basis_ref,
    z_ref, v_ref, sums_ref, mixed_ref, partial_ref, modal_ref,
):
    mask = live_mask(count_ref[0])
    sums = jnp.sum(gathered_ref[...], axis=0, keepdims=True)
    sums_ref[...] = jnp.broadcast_to(sums, sums_ref.shape)
    along = lane_of(sums, MODES) / lane_of(sums, MODES + 2)
    scale = 1.0 / jnp.sqrt(lane_of(sums, MODES + 1))
    mixed_ref[...] = (halves(gathered_ref) - along * coarse_ref[...]) * scale
    v_ref[...] = (w_ref[...] - along * b_ref[...]) * scale
    z = precondition(v_ref, mixed_ref, inverse_ref, local_ref, basis_ref, partial_ref, modal_ref)
    z_ref[...] = z * mask


def face_of(q):
    if q < 2:
        odd = lax.rem(lax.axis_index("gx"), 2)
        return 1 - odd if q == 0 else odd
    odd = lax.rem(lax.axis_index("gy"), 2)
    return 3 - odd if q == 2 else 2 + odd


def pick(source_ref, partners_ref, q):
    slots = jnp.broadcast_to(partners_ref[pl.ds(face_of(q), 1), :], (NODES, SLOTS))
    return jnp.take_along_axis(source_ref[...], slots, axis=1)


def own_kernel(
    z_ref, blocks_ref, pressure_ref, alpha_ref, partners_ref, s0, faces_ref, out_ref, picked_ref, partial_ref
):
    picked_ref[0] = pick(s0, partners_ref, 0)
    face = face_of(0)
    blocks_into(
        partial_ref,
        [(lambda i: blocks_ref[i], lambda: z_ref[...]), (lambda i: faces_ref[face, i], lambda: picked_ref[0])],
    )
    alpha = alpha_ref[...]
    scaled = jnp.abs(alpha * pressure_ref[...])
    power = jnp.exp((shape_exponent - 1.0) * jnp.log(scaled))
    tail = jnp.exp(-(expo_m + 1.0) * jnp.log(1.0 + power * scaled))
    storage = (time_factor * shape_exponent * expo_m) * alpha * power * tail
    out_ref[...] = fold_rows(partial_ref, NODES) + storage * z_ref[...]


def faces_sum(own_ref, count_ref, partners_ref, source_refs, blocks_ref, picked_ref, partial_ref):
    terms = []
    for q, source_ref in enumerate(source_refs):
        picked_ref[q] = pick(source_ref, partners_ref, q + 1)
        face = face_of(q + 1)
        terms.append((lambda i, face=face: blocks_ref[face, i], lambda q=q: picked_ref[q]))
    blocks_into(partial_ref, terms)
    return (own_ref[...] + fold_rows(partial_ref, NODES)) * live_mask(count_ref[0])


def image_kernel(
    own_ref, count_ref, partners_ref, s1, s2, s3, blocks_ref, b_ref, basis_ref,
    w_ref, row_ref, picked_ref, partial_ref,
):
    w_ref[...] = faces_sum(
        own_ref, count_ref, partners_ref, (s1, s2, s3), blocks_ref, picked_ref, partial_ref
    )
    blocks_into(partial_ref, [(lambda m: basis_ref[m], lambda: w_ref[...])])
    w = w_ref[...]
    b = b_ref[...]
    put_dots(partial_ref, [(w, b), (w, w), (b, b)])
    send_row(partial_ref, row_ref)


def last_image_kernel(
    own_ref, count_ref, partners_ref, s1, s2, s3, blocks_ref, b_ref, v_ref,
    row_ref, picked_ref, partial_ref,
):
    w = faces_sum(
        own_ref, count_ref, partners_ref, (s1, s2, s3), blocks_ref, picked_ref, partial_ref
    )
    b = b_ref[...]
    v = v_ref[...]
    partial_ref[pl.ds(0, 8 * MODES), :] = jnp.zeros((8 * MODES, SLOTS), F32)
    put_dots(partial_ref, [(w, b), (w, v), (w, w), (v, v), (b, v)])
    send_row(partial_ref, row_ref)


def final_kernel(first_ref, gathered_ref, z1_ref, z2_ref, update_ref, hess_ref):
    sums = first_ref[0:1, :]
    late = jnp.sum(gathered_ref[...], axis=0, keepdims=True)
    wb, ww, bb = (lane_of(sums, MODES + k) for k in range(3))
    xb, xv, xx, vv, bv = (lane_of(late, MODES + k) for k in range(5))
    beta = jnp.sqrt(bb)
    size = jnp.sqrt(vv)
    h11 = wb / bb
    h21 = size * jnp.sqrt(ww) / beta
    h12 = xb / (size * beta)
    h22 = xv / vv
    cross = bv / (beta * size)
    rest = xx / vv - h12 * h12 - h22 * h22 + 2.0 * h12 * h22 * cross
    h32 = jnp.sqrt(jnp.maximum(rest, 0.0))
    gram_aa = h11 * h11 + h21 * h21
    gram_ab = h11 * h12 + h21 * h22
    gram_bb = h12 * h12 + h22 * h22 + h32 * h32
    target_a = beta * h11
    target_b = beta * h12
    determinant = gram_aa * gram_bb - gram_ab * gram_ab
    weight_one = (gram_bb * target_a - gram_ab * target_b) / determinant
    weight_two = (gram_aa * target_b - gram_ab * target_a) / determinant
    update_ref[...] = (weight_one / beta) * z1_ref[...] + (weight_two / size) * z2_ref[...]
    row = lax.broadcasted_iota(jnp.int32, (2, 3), 0)
    col = lax.broadcasted_iota(jnp.int32, (2, 3), 1)
    hess = jnp.where(row == 0, jnp.where(col == 0, h11, h21), jnp.where(col == 0, h12, jnp.where(col == 1, h22, h32)))
    hess_ref[...] = jnp.where((row == 0) & (col == 2), 0.0, hess)


def vec(*shape):
    return jax.ShapeDtypeStruct(shape, F32)


def call(body, name, specs, outs, scratch, megabytes=4):
    return pl.pallas_call(
        body,
        name=name,
        in_specs=specs,
        out_specs=jax.tree.map(lambda _: VM, outs),
        out_shape=outs,
        scratch_shapes=scratch,
        compiler_params=pltpu.CompilerParams(vmem_limit_bytes=megabytes << 20),
    )


def swaps(mesh_shape):
    n_gx, n_gy = mesh_shape
    at = lambda i, j: i * n_gy + j
    pairs = ([], [], [], [])
    for i in range(n_gx):
        for j in range(n_gy):
            if i + 1 < n_gx:
                pairs[i % 2].extend([(at(i, j), at(i + 1, j)), (at(i + 1, j), at(i, j))])
            if j + 1 < n_gy:
                pairs[2 + j % 2].extend([(at(i, j), at(i, j + 1)), (at(i, j + 1), at(i, j))])
    return pairs


def solution(mesh):
    axes = ("gx", "gy")
    n_gx, n_gy = mesh.shape["gx"], mesh.shape["gy"]
    total = n_gx * n_gy
    pairs = swaps((n_gx, n_gy))

    def exchange(rows):
        return lax.all_to_all(rows, axes, 0, 0, tiled=True)

    def shards(
        right_side, pressure_head, vg_alpha, live_counts, partners,
        element_blocks, face_blocks, local_inverse, coarse_basis, coarse_inverse,
    ):
        alpha = vg_alpha.reshape(1, SLOTS)
        partial = pltpu.VMEM((8 * ROWS, SLOTS), F32)
        picked = pltpu.VMEM((3, NODES, SLOTS), F32)
        modal = pltpu.VMEM((MODES, SLOTS), F32)

        in_hbm = lambda x: pltpu.with_memory_space_constraint(x, pltpu.HBM)
        held = lambda x: jax.ShapeDtypeStruct(x.shape, x.dtype)
        semaphore = pltpu.SemaphoreType.DMA
        rows, b, basis, local, inverse = call(
            restrict_kernel, "restrict", [SM] + [HB] * 4,
            (vec(total, SLOTS), held(right_side), held(coarse_basis), held(local_inverse), held(coarse_inverse)),
            [partial, semaphore, semaphore((PIECES,)), semaphore, semaphore],
        )(live_counts, *(in_hbm(x) for x in (right_side, coarse_basis, local_inverse, coarse_inverse)))
        gathered = exchange(rows)
        z1, coarse = call(
            first_kernel, "first", [SM] + [VM] * 5,
            (vec(NODES, SLOTS), vec(SLOTS, SLOTS)), [partial, modal],
        )(live_counts, b, gathered, inverse, local, basis)

        def neighbours(z):
            sources = [None] * 4
            for q in ORDER:
                sources[q] = lax.ppermute(z, axes, pairs[q])
            return sources

        def own(z, source):
            return call(own_kernel, "own", [VM] * 7, vec(NODES, SLOTS), [pltpu.VMEM((1, NODES, SLOTS), F32), partial])(
                z, element_blocks, pressure_head, alpha, partners, source, face_blocks
            )

        sources = neighbours(z1)
        w1, rows = call(
            image_kernel, "image", [VM, SM] + [VM] * 7,
            (vec(NODES, SLOTS), vec(total, SLOTS)), [picked, partial],
        )(own(z1, sources[0]), live_counts, partners, *sources[1:], face_blocks, b, basis)
        gathered = exchange(rows)
        z2, v2, sums = call(
            second_kernel, "second", [VM, VM, SM] + [VM] * 5,
            (vec(NODES, SLOTS), vec(NODES, SLOTS), vec(8, SLOTS)),
            [pltpu.VMEM((SLOTS, SLOTS), F32), partial, modal],
        )(b, w1, live_counts, coarse, gathered, inverse, local, basis)
        sources = neighbours(z2)
        rows = call(
            last_image_kernel, "last_image", [VM, SM] + [VM] * 7,
            vec(total, SLOTS), [picked, partial],
        )(own(z2, sources[0]), live_counts, partners, *sources[1:], face_blocks, b, v2)
        gathered = exchange(rows)
        update, hess = call(
            final_kernel, "final", [VM] * 4, (vec(NODES, SLOTS), vec(2, 3)), []
        )(sums, gathered, z1, z2)
        return update, hess.T

    placed = (
        P(None, axes), P(None, axes), P(axes), P(axes), P(None, axes),
        P(None, None, axes), P(None, None, None, axes), P(None, None, axes), P(None, None, axes),
        P(axes, None),
    )
    return jax.shard_map(
        shards, mesh=mesh, in_specs=placed, out_specs=(P(None, axes), P()), check_vma=False
    )
```

```python
import jax
import jax.numpy as jnp
from jax import lax
from jax.experimental import pallas as pl
from jax.experimental.pallas import tpu as pltpu
from jax.sharding import PartitionSpec as P

shape_exponent = 1.6
time_factor = 4.0
expo_m = 1.0 - 1.0 / shape_exponent

NODES = 64
MODES = 64
SLOTS = 128
DOTS = 8
ROWS = MODES + DOTS
F32 = jnp.float32
VM = pl.BlockSpec(memory_space=pltpu.VMEM)
HB = pl.BlockSpec(memory_space=pltpu.HBM)
PIECES = 4
UNROLL = 8
EARLY = (2, 1, 0)
LATER = (3,)


def live_mask(count):
    slots = lax.broadcasted_iota(jnp.int32, (8, SLOTS), 1)
    return (slots < count).astype(F32)


def tile_sum(block):
    parts = [block[8 * t : 8 * t + 8] for t in range(8)]
    while len(parts) > 1:
        parts = [a + b for a, b in zip(parts[::2], parts[1::2])]
    return parts[0]


def fold_rows(partial_ref, rows):
    parts = [partial_ref[pl.ds(k, rows, stride=8), :] for k in range(8)]
    while len(parts) > 1:
        parts = [a + b for a, b in zip(parts[::2], parts[1::2])]
    return parts[0]


def blocks_into(partial_ref, terms, first=0, last=NODES):
    def body(i, carry):
        total = None
        for block_at, vector in terms:
            part = tile_sum(block_at(i).astype(F32) * vector())
            total = part if total is None else total + part
        partial_ref[pl.ds(pl.multiple_of(8 * i, 8), 8), :] = total
        return carry

    lax.fori_loop(first, last, body, 0, unroll=UNROLL)


def send_row(partial_ref, out_ref):
    square = jnp.concatenate(
        [fold_rows(partial_ref, ROWS), jnp.zeros((SLOTS - ROWS, SLOTS), F32)], axis=0
    )
    row = jnp.sum(square.T, axis=0, keepdims=True)
    out_ref[...] = jnp.broadcast_to(row, out_ref.shape)


def put_dots(partial_ref, pairs):
    for k in range(DOTS):
        rows = pl.ds(8 * (MODES + k), 8)
        if k < len(pairs):
            left, right = pairs[k]
            partial_ref[rows, :] = tile_sum(left * right)
        else:
            partial_ref[rows, :] = jnp.zeros((8, SLOTS), F32)


def restrict_kernel(
    count_ref, rhs_hbm, basis_hbm, local_hbm, inverse_hbm,
    row_ref, b_ref, mask_ref, basis_ref, local_ref, inverse_ref,
    partial_ref, rhs_sem, basis_sem, local_sem, inverse_sem,
):
    rhs_copy = pltpu.make_async_copy(rhs_hbm, b_ref, rhs_sem)
    rhs_copy.start()
    modes = MODES // PIECES
    copies = []
    for k in range(PIECES):
        piece = pl.ds(k * modes, modes)
        copies.append(pltpu.make_async_copy(basis_hbm.at[piece], basis_ref.at[piece], basis_sem.at[k]))
        copies[-1].start()
    local_copy = pltpu.make_async_copy(local_hbm, local_ref, local_sem)
    local_copy.start()
    inverse_copy = pltpu.make_async_copy(inverse_hbm, inverse_ref, inverse_sem)
    inverse_copy.start()
    put_dots(partial_ref, [])
    mask_ref[...] = live_mask(count_ref[0])
    rhs_copy.wait()
    b_ref[...] = b_ref[...] * mask_ref[0:1, :]
    for k, copy in enumerate(copies):
        copy.wait()
        blocks_into(
            partial_ref, [(lambda m: basis_ref[m], lambda: b_ref[...])], k * modes, (k + 1) * modes
        )
    send_row(partial_ref, row_ref)
    local_copy.wait()
    inverse_copy.wait()


def halves(rows_ref):
    lane = lax.broadcasted_iota(jnp.int32, (SLOTS, SLOTS), 1)
    even = rows_ref[pl.ds(0, SLOTS, stride=2), :]
    odd = rows_ref[pl.ds(1, SLOTS, stride=2), :]
    return jnp.where(lane < MODES, even, pltpu.roll(odd, MODES, 1))


def precondition(v_ref, coarse_ref, inverse_ref, local_ref, basis_ref, partial_ref, modal_ref):
    def coarse_step(t, acc):
        column = inverse_ref[:, pl.ds(pl.multiple_of(t * SLOTS, SLOTS), SLOTS)].astype(F32)
        return acc + column * coarse_ref[pl.ds(t, 1), :]

    acc = lax.fori_loop(0, 2 * MODES, coarse_step, jnp.zeros((MODES, SLOTS), F32), unroll=2 * UNROLL)
    modal_ref[...] = jnp.broadcast_to(jnp.sum(acc, axis=1, keepdims=True), (MODES, SLOTS))
    blocks_into(partial_ref, [(lambda i: local_ref[i], lambda: v_ref[...])])

    def prolong_step(m, total):
        return total + basis_ref[m].astype(F32) * modal_ref[pl.ds(m, 1), :]

    total = lax.fori_loop(0, MODES, prolong_step, jnp.zeros((NODES, SLOTS), F32), unroll=2 * UNROLL)
    return total + fold_rows(partial_ref, NODES)


def first_kernel(
    mask_ref, b_ref, gathered_ref, inverse_ref, local_ref, basis_ref,
    z_ref, coarse_ref, partial_ref, modal_ref,
):
    coarse_ref[...] = halves(gathered_ref)
    z = precondition(b_ref, coarse_ref, inverse_ref, local_ref, basis_ref, partial_ref, modal_ref)
    z_ref[...] = z * mask_ref[0:1, :]


def lane_of(row, k):
    lane = lax.broadcasted_iota(jnp.int32, row.shape, 1)
    return jnp.sum(jnp.where(lane == k, row, 0.0), axis=1, keepdims=True)


def second_kernel(
    b_ref, w_ref, mask_ref, coarse_ref, gathered_ref, inverse_ref, local_ref, basis_ref,
    z_ref, v_ref, sums_ref, mixed_ref, partial_ref, modal_ref,
):
    sums = jnp.sum(gathered_ref[...], axis=0, keepdims=True)
    sums_ref[...] = jnp.broadcast_to(sums, sums_ref.shape)
    along = lane_of(sums, MODES) / lane_of(sums, MODES + 2)
    scale = 1.0 / jnp.sqrt(lane_of(sums, MODES + 1))
    mixed_ref[...] = (halves(gathered_ref) - along * coarse_ref[...]) * scale
    v_ref[...] = (w_ref[...] - along * b_ref[...]) * scale
    z = precondition(v_ref, mixed_ref, inverse_ref, local_ref, basis_ref, partial_ref, modal_ref)
    z_ref[...] = z * mask_ref[0:1, :]


def face_of(q):
    if q < 2:
        odd = lax.rem(lax.axis_index("gx"), 2)
        return 1 - odd if q == 0 else odd
    odd = lax.rem(lax.axis_index("gy"), 2)
    return 3 - odd if q == 2 else 2 + odd


def pick(source_ref, partners_ref, q):
    slots = jnp.broadcast_to(partners_ref[pl.ds(face_of(q), 1), :], (NODES, SLOTS))
    return jnp.take_along_axis(source_ref[...], slots, axis=1)


def face_terms(qs, source_refs, partners_ref, faces_ref, picked_ref):
    terms = []
    for k, (q, source_ref) in enumerate(zip(qs, source_refs)):
        picked_ref[k] = pick(source_ref, partners_ref, q)
        face = face_of(q)
        terms.append((lambda i, face=face: faces_ref[face, i], lambda k=k: picked_ref[k]))
    return terms


def own_kernel(
    z_ref, blocks_ref, pressure_ref, alpha_ref, partners_ref, s0, s1, s2, faces_ref, out_ref, picked_ref, partial_ref
):
    terms = face_terms(EARLY, (s0, s1, s2), partners_ref, faces_ref, picked_ref)
    blocks_into(partial_ref, [(lambda i: blocks_ref[i], lambda: z_ref[...])] + terms)
    alpha = alpha_ref[...]
    scaled = jnp.abs(alpha * pressure_ref[...])
    power = jnp.exp((shape_exponent - 1.0) * jnp.log(scaled))
    tail = jnp.exp(-(expo_m + 1.0) * jnp.log(1.0 + power * scaled))
    storage = (time_factor * shape_exponent * expo_m) * alpha * power * tail
    out_ref[...] = fold_rows(partial_ref, NODES) + storage * z_ref[...]


def all_blocks(own_ref, mask_ref, partners_ref, source_ref, faces_ref, picked_ref, partial_ref):
    blocks_into(partial_ref, face_terms(LATER, (source_ref,), partners_ref, faces_ref, picked_ref))
    return (own_ref[...] + fold_rows(partial_ref, NODES)) * mask_ref[0:1, :]


def image_kernel(
    own_ref, mask_ref, partners_ref, s3, blocks_ref, b_ref, basis_ref,
    w_ref, row_ref, picked_ref, partial_ref,
):
    w_ref[...] = all_blocks(own_ref, mask_ref, partners_ref, s3, blocks_ref, picked_ref, partial_ref)
    blocks_into(partial_ref, [(lambda m: basis_ref[m], lambda: w_ref[...])])
    w = w_ref[...]
    b = b_ref[...]
    put_dots(partial_ref, [(w, b), (w, w), (b, b)])
    send_row(partial_ref, row_ref)


def last_image_kernel(
    own_ref, mask_ref, partners_ref, s3, blocks_ref, b_ref, v_ref,
    row_ref, picked_ref, partial_ref,
):
    w = all_blocks(own_ref, mask_ref, partners_ref, s3, blocks_ref, picked_ref, partial_ref)
    b = b_ref[...]
    v = v_ref[...]
    partial_ref[pl.ds(0, 8 * MODES), :] = jnp.zeros((8 * MODES, SLOTS), F32)
    put_dots(partial_ref, [(w, b), (w, v), (w, w), (v, v), (b, v)])
    send_row(partial_ref, row_ref)


def final_kernel(first_ref, gathered_ref, z1_ref, z2_ref, update_ref, hess_ref):
    sums = first_ref[0:1, :]
    late = jnp.sum(gathered_ref[...], axis=0, keepdims=True)
    wb, ww, bb = (lane_of(sums, MODES + k) for k in range(3))
    xb, xv, xx, vv, bv = (lane_of(late, MODES + k) for k in range(5))
    beta = jnp.sqrt(bb)
    size = jnp.sqrt(vv)
    h11 = wb / bb
    h21 = size * jnp.sqrt(ww) / beta
    h12 = xb / (size * beta)
    h22 = xv / vv
    cross = bv / (beta * size)
    rest = xx / vv - h12 * h12 - h22 * h22 + 2.0 * h12 * h22 * cross
    h32 = jnp.sqrt(jnp.maximum(rest, 0.0))
    gram_aa = h11 * h11 + h21 * h21
    gram_ab = h11 * h12 + h21 * h22
    gram_bb = h12 * h12 + h22 * h22 + h32 * h32
    target_a = beta * h11
    target_b = beta * h12
    determinant = gram_aa * gram_bb - gram_ab * gram_ab
    weight_one = (gram_bb * target_a - gram_ab * target_b) / determinant
    weight_two = (gram_aa * target_b - gram_ab * target_a) / determinant
    update_ref[...] = (weight_one / beta) * z1_ref[...] + (weight_two / size) * z2_ref[...]
    row = lax.broadcasted_iota(jnp.int32, (2, 3), 0)
    col = lax.broadcasted_iota(jnp.int32, (2, 3), 1)
    hess = jnp.where(row == 0, jnp.where(col == 0, h11, h21), jnp.where(col == 0, h12, jnp.where(col == 1, h22, h32)))
    hess_ref[...] = jnp.where((row == 0) & (col == 2), 0.0, hess)


def vec(*shape):
    return jax.ShapeDtypeStruct(shape, F32)


def call(body, name, specs, outs, scratch, megabytes=4):
    return pl.pallas_call(
        body,
        name=name,
        in_specs=specs,
        out_specs=jax.tree.map(lambda _: VM, outs),
        out_shape=outs,
        scratch_shapes=scratch,
        compiler_params=pltpu.CompilerParams(vmem_limit_bytes=megabytes << 20),
    )


def swaps(mesh_shape):
    n_gx, n_gy = mesh_shape
    at = lambda i, j: i * n_gy + j
    pairs = ([], [], [], [])
    for i in range(n_gx):
        for j in range(n_gy):
            if i + 1 < n_gx:
                pairs[i % 2].extend([(at(i, j), at(i + 1, j)), (at(i + 1, j), at(i, j))])
            if j + 1 < n_gy:
                pairs[2 + j % 2].extend([(at(i, j), at(i, j + 1)), (at(i, j + 1), at(i, j))])
    return pairs


def solution(mesh):
    axes = ("gx", "gy")
    n_gx, n_gy = mesh.shape["gx"], mesh.shape["gy"]
    total = n_gx * n_gy
    pairs = swaps((n_gx, n_gy))

    def exchange(rows):
        return lax.all_to_all(rows, axes, 0, 0, tiled=True)

    def shards(
        right_side, pressure_head, vg_alpha, live_counts, partners,
        element_blocks, face_blocks, local_inverse, coarse_basis, coarse_inverse,
    ):
        alpha = vg_alpha.reshape(1, SLOTS)
        partial = pltpu.VMEM((8 * ROWS, SLOTS), F32)
        picked = pltpu.VMEM((3, NODES, SLOTS), F32)
        modal = pltpu.VMEM((MODES, SLOTS), F32)

        in_hbm = lambda x: pltpu.with_memory_space_constraint(x, pltpu.HBM)
        held = lambda x: jax.ShapeDtypeStruct(x.shape, x.dtype)
        semaphore = pltpu.SemaphoreType.DMA
        rows, b, mask, basis, local, inverse = call(
            restrict_kernel, "restrict", [pl.BlockSpec(memory_space=pltpu.SMEM)] + [HB] * 4,
            (vec(total, SLOTS), held(right_side), vec(8, SLOTS), held(coarse_basis), held(local_inverse), held(coarse_inverse)),
            [partial, semaphore, semaphore((PIECES,)), semaphore, semaphore],
        )(live_counts, *(in_hbm(x) for x in (right_side, coarse_basis, local_inverse, coarse_inverse)))
        gathered = exchange(rows)
        z1, coarse = call(
            first_kernel, "first", [VM] * 6,
            (vec(NODES, SLOTS), vec(SLOTS, SLOTS)), [partial, modal],
        )(mask, b, gathered, inverse, local, basis)

        def neighbours(z):
            return [lax.ppermute(z, axes, pairs[q]) for q in EARLY + LATER]

        def own(z, sources):
            return call(own_kernel, "own", [VM] * 9, vec(NODES, SLOTS), [picked, partial])(
                z, element_blocks, pressure_head, alpha, partners, *sources, face_blocks
            )

        sources = neighbours(z1)
        w1, rows = call(
            image_kernel, "image", [VM] * 7,
            (vec(NODES, SLOTS), vec(total, SLOTS)), [picked, partial],
        )(own(z1, sources[:3]), mask, partners, sources[3], face_blocks, b, basis)
        gathered = exchange(rows)
        z2, v2, sums = call(
            second_kernel, "second", [VM] * 8,
            (vec(NODES, SLOTS), vec(NODES, SLOTS), vec(8, SLOTS)),
            [pltpu.VMEM((SLOTS, SLOTS), F32), partial, modal],
        )(b, w1, mask, coarse, gathered, inverse, local, basis)
        sources = neighbours(z2)
        rows = call(
            last_image_kernel, "last_image", [VM] * 7,
            vec(total, SLOTS), [picked, partial],
        )(own(z2, sources[:3]), mask, partners, sources[3], face_blocks, b, v2)
        gathered = exchange(rows)
        update, hess = call(
            final_kernel, "final", [VM] * 4, (vec(NODES, SLOTS), vec(2, 3)), []
        )(sums, gathered, z1, z2)
        return update, hess.T

    placed = (
        P(None, axes), P(None, axes), P(axes), P(axes), P(None, axes),
        P(None, None, axes), P(None, None, None, axes), P(None, None, axes), P(None, None, axes),
        P(axes, None),
    )
    return jax.shard_map(
        shards, mesh=mesh, in_specs=placed, out_specs=(P(None, axes), P()), check_vma=False
    )
```

```python
import jax
import jax.numpy as jnp
from jax import lax
from jax.experimental import pallas as pl
from jax.experimental.pallas import tpu as pltpu
from jax.sharding import PartitionSpec as P

shape_exponent = 1.6
time_factor = 4.0
expo_m = 1.0 - 1.0 / shape_exponent

NODES = 64
MODES = 64
SLOTS = 128
DOTS = 8
ROWS = MODES + DOTS
F32 = jnp.float32
VM = pl.BlockSpec(memory_space=pltpu.VMEM)
HB = pl.BlockSpec(memory_space=pltpu.HBM)
PIECES = 4
UNROLL = 8
EARLY = (2, 1, 0)
LATER = (3,)


def live_mask(count):
    slots = lax.broadcasted_iota(jnp.int32, (8, SLOTS), 1)
    return (slots < count).astype(F32)


def tile_sum(block):
    parts = [block[8 * t : 8 * t + 8] for t in range(8)]
    while len(parts) > 1:
        parts = [a + b for a, b in zip(parts[::2], parts[1::2])]
    return parts[0]


def fold_rows(partial_ref, rows):
    parts = [partial_ref[pl.ds(k, rows, stride=8), :] for k in range(8)]
    while len(parts) > 1:
        parts = [a + b for a, b in zip(parts[::2], parts[1::2])]
    return parts[0]


def blocks_into(partial_ref, terms, first=0, last=NODES):
    def body(i, carry):
        total = None
        for block_at, vector in terms:
            part = tile_sum(block_at(i).astype(F32) * vector())
            total = part if total is None else total + part
        partial_ref[pl.ds(pl.multiple_of(8 * i, 8), 8), :] = total
        return carry

    lax.fori_loop(first, last, body, 0, unroll=UNROLL)


def send_row(partial_ref, out_ref):
    square = jnp.concatenate(
        [fold_rows(partial_ref, ROWS), jnp.zeros((SLOTS - ROWS, SLOTS), F32)], axis=0
    )
    row = jnp.sum(square.T, axis=0, keepdims=True)
    out_ref[...] = jnp.broadcast_to(row, out_ref.shape)


def put_dots(partial_ref, pairs):
    for k in range(DOTS):
        rows = pl.ds(8 * (MODES + k), 8)
        if k < len(pairs):
            left, right = pairs[k]
            partial_ref[rows, :] = tile_sum(left * right)
        else:
            partial_ref[rows, :] = jnp.zeros((8, SLOTS), F32)


def apply_local(local_ref, v_ref, partial_ref):
    blocks_into(partial_ref, [(lambda i: local_ref[i], lambda: v_ref[...])])
    return fold_rows(partial_ref, NODES)


def restrict_kernel(
    count_ref, rhs_hbm, basis_hbm, local_hbm, inverse_hbm,
    row_ref, b_ref, mask_ref, local_b_ref, basis_ref, local_ref, inverse_ref,
    partial_ref, other_ref, rhs_sem, basis_sem, local_sem, inverse_sem,
):
    rhs_copy = pltpu.make_async_copy(rhs_hbm, b_ref, rhs_sem)
    rhs_copy.start()
    modes = MODES // PIECES
    copies = []
    for k in range(PIECES):
        piece = pl.ds(k * modes, modes)
        copies.append(pltpu.make_async_copy(basis_hbm.at[piece], basis_ref.at[piece], basis_sem.at[k]))
        copies[-1].start()
    local_copy = pltpu.make_async_copy(local_hbm, local_ref, local_sem)
    local_copy.start()
    inverse_copy = pltpu.make_async_copy(inverse_hbm, inverse_ref, inverse_sem)
    inverse_copy.start()
    put_dots(partial_ref, [])
    mask_ref[...] = live_mask(count_ref[0])
    rhs_copy.wait()
    b_ref[...] = b_ref[...] * mask_ref[0:1, :]
    for k, copy in enumerate(copies):
        copy.wait()
        blocks_into(
            partial_ref, [(lambda m: basis_ref[m], lambda: b_ref[...])], k * modes, (k + 1) * modes
        )
    send_row(partial_ref, row_ref)
    local_copy.wait()
    local_b_ref[...] = apply_local(local_ref, b_ref, other_ref)
    inverse_copy.wait()


def halves(rows_ref):
    lane = lax.broadcasted_iota(jnp.int32, (SLOTS, SLOTS), 1)
    even = rows_ref[pl.ds(0, SLOTS, stride=2), :]
    odd = rows_ref[pl.ds(1, SLOTS, stride=2), :]
    return jnp.where(lane < MODES, even, pltpu.roll(odd, MODES, 1))


def coarse_part(start, coarse_ref, inverse_ref, basis_ref, modal_ref):
    def coarse_step(t, acc):
        column = inverse_ref[:, pl.ds(pl.multiple_of(t * SLOTS, SLOTS), SLOTS)].astype(F32)
        return acc + column * coarse_ref[pl.ds(t, 1), :]

    acc = lax.fori_loop(0, 2 * MODES, coarse_step, jnp.zeros((MODES, SLOTS), F32), unroll=2 * UNROLL)
    modal_ref[...] = jnp.broadcast_to(jnp.sum(acc, axis=1, keepdims=True), (MODES, SLOTS))

    def prolong_step(m, total):
        return total + basis_ref[m].astype(F32) * modal_ref[pl.ds(m, 1), :]

    return lax.fori_loop(0, MODES, prolong_step, start, unroll=2 * UNROLL)


def first_kernel(
    mask_ref, local_b_ref, gathered_ref, inverse_ref, basis_ref, z_ref, coarse_ref, modal_ref
):
    coarse_ref[...] = halves(gathered_ref)
    z = coarse_part(local_b_ref[...], coarse_ref, inverse_ref, basis_ref, modal_ref)
    z_ref[...] = z * mask_ref[0:1, :]


def lane_of(row, k):
    lane = lax.broadcasted_iota(jnp.int32, row.shape, 1)
    return jnp.sum(jnp.where(lane == k, row, 0.0), axis=1, keepdims=True)


def second_kernel(
    b_ref, w_ref, mask_ref, z1_ref, gathered_ref, inverse_ref, local_ref, basis_ref,
    z_ref, v_ref, sums_ref, coarse_ref, partial_ref, modal_ref,
):
    sums = jnp.sum(gathered_ref[...], axis=0, keepdims=True)
    sums_ref[...] = jnp.broadcast_to(sums, sums_ref.shape)
    along = lane_of(sums, MODES) / lane_of(sums, MODES + 2)
    scale = 1.0 / jnp.sqrt(lane_of(sums, MODES + 1))
    v_ref[...] = (w_ref[...] - along * b_ref[...]) * scale
    coarse_ref[...] = halves(gathered_ref)
    local_part = apply_local(local_ref, w_ref, partial_ref)
    z = coarse_part(local_part, coarse_ref, inverse_ref, basis_ref, modal_ref)
    z_ref[...] = (z * mask_ref[0:1, :] - along * z1_ref[...]) * scale


def face_of(q):
    if q < 2:
        odd = lax.rem(lax.axis_index("gx"), 2)
        return 1 - odd if q == 0 else odd
    odd = lax.rem(lax.axis_index("gy"), 2)
    return 3 - odd if q == 2 else 2 + odd


def pick(source_ref, partners_ref, q):
    slots = jnp.broadcast_to(partners_ref[pl.ds(face_of(q), 1), :], (NODES, SLOTS))
    return jnp.take_along_axis(source_ref[...], slots, axis=1)


def face_terms(qs, source_refs, partners_ref, faces_ref, picked_ref):
    terms = []
    for k, (q, source_ref) in enumerate(zip(qs, source_refs)):
        picked_ref[k] = pick(source_ref, partners_ref, q)
        face = face_of(q)
        terms.append((lambda i, face=face: faces_ref[face, i], lambda k=k: picked_ref[k]))
    return terms


def own_kernel(z_ref, blocks_ref, pressure_ref, alpha_ref, partners_ref, *refs):
    source_refs, (faces_ref, out_ref, picked_ref, partial_ref) = refs[: len(EARLY)], refs[len(EARLY) :]
    terms = face_terms(EARLY, source_refs, partners_ref, faces_ref, picked_ref)
    blocks_into(partial_ref, [(lambda i: blocks_ref[i], lambda: z_ref[...])] + terms)
    alpha = alpha_ref[...]
    scaled = jnp.abs(alpha * pressure_ref[...])
    power = jnp.exp((shape_exponent - 1.0) * jnp.log(scaled))
    tail = jnp.exp(-(expo_m + 1.0) * jnp.log(1.0 + power * scaled))
    storage = (time_factor * shape_exponent * expo_m) * alpha * power * tail
    out_ref[...] = fold_rows(partial_ref, NODES) + storage * z_ref[...]


def all_blocks(own_ref, mask_ref, partners_ref, source_refs, faces_ref, picked_ref, partial_ref):
    blocks_into(partial_ref, face_terms(LATER, source_refs, partners_ref, faces_ref, picked_ref))
    return (own_ref[...] + fold_rows(partial_ref, NODES)) * mask_ref[0:1, :]


def image_kernel(own_ref, mask_ref, partners_ref, *refs):
    source_refs, refs = refs[: len(LATER)], refs[len(LATER) :]
    blocks_ref, b_ref, basis_ref, w_ref, row_ref, picked_ref, partial_ref = refs
    w_ref[...] = all_blocks(own_ref, mask_ref, partners_ref, source_refs, blocks_ref, picked_ref, partial_ref)
    blocks_into(partial_ref, [(lambda m: basis_ref[m], lambda: w_ref[...])])
    w = w_ref[...]
    b = b_ref[...]
    put_dots(partial_ref, [(w, b), (w, w), (b, b)])
    send_row(partial_ref, row_ref)


def last_image_kernel(own_ref, mask_ref, partners_ref, *refs):
    source_refs, refs = refs[: len(LATER)], refs[len(LATER) :]
    blocks_ref, b_ref, v_ref, row_ref, picked_ref, partial_ref = refs
    w = all_blocks(own_ref, mask_ref, partners_ref, source_refs, blocks_ref, picked_ref, partial_ref)
    b = b_ref[...]
    v = v_ref[...]
    partial_ref[pl.ds(0, 8 * MODES), :] = jnp.zeros((8 * MODES, SLOTS), F32)
    put_dots(partial_ref, [(w, b), (w, v), (w, w), (v, v), (b, v)])
    send_row(partial_ref, row_ref)


def final_kernel(first_ref, gathered_ref, z1_ref, z2_ref, update_ref, hess_ref):
    sums = first_ref[0:1, :]
    late = jnp.sum(gathered_ref[...], axis=0, keepdims=True)
    wb, ww, bb = (lane_of(sums, MODES + k) for k in range(3))
    xb, xv, xx, vv, bv = (lane_of(late, MODES + k) for k in range(5))
    beta = jnp.sqrt(bb)
    size = jnp.sqrt(vv)
    h11 = wb / bb
    h21 = size * jnp.sqrt(ww) / beta
    h12 = xb / (size * beta)
    h22 = xv / vv
    cross = bv / (beta * size)
    rest = xx / vv - h12 * h12 - h22 * h22 + 2.0 * h12 * h22 * cross
    h32 = jnp.sqrt(jnp.maximum(rest, 0.0))
    gram_aa = h11 * h11 + h21 * h21
    gram_ab = h11 * h12 + h21 * h22
    gram_bb = h12 * h12 + h22 * h22 + h32 * h32
    target_a = beta * h11
    target_b = beta * h12
    determinant = gram_aa * gram_bb - gram_ab * gram_ab
    weight_one = (gram_bb * target_a - gram_ab * target_b) / determinant
    weight_two = (gram_aa * target_b - gram_ab * target_a) / determinant
    update_ref[...] = (weight_one / beta) * z1_ref[...] + (weight_two / size) * z2_ref[...]
    row = lax.broadcasted_iota(jnp.int32, (2, 3), 0)
    col = lax.broadcasted_iota(jnp.int32, (2, 3), 1)
    hess = jnp.where(row == 0, jnp.where(col == 0, h11, h21), jnp.where(col == 0, h12, jnp.where(col == 1, h22, h32)))
    hess_ref[...] = jnp.where((row == 0) & (col == 2), 0.0, hess)


def vec(*shape):
    return jax.ShapeDtypeStruct(shape, F32)


def call(body, name, specs, outs, scratch, megabytes=4):
    return pl.pallas_call(
        body,
        name=name,
        in_specs=specs,
        out_specs=jax.tree.map(lambda _: VM, outs),
        out_shape=outs,
        scratch_shapes=scratch,
        compiler_params=pltpu.CompilerParams(vmem_limit_bytes=megabytes << 20),
    )


def swaps(mesh_shape):
    n_gx, n_gy = mesh_shape
    at = lambda i, j: i * n_gy + j
    pairs = ([], [], [], [])
    for i in range(n_gx):
        for j in range(n_gy):
            if i + 1 < n_gx:
                pairs[i % 2].extend([(at(i, j), at(i + 1, j)), (at(i + 1, j), at(i, j))])
            if j + 1 < n_gy:
                pairs[2 + j % 2].extend([(at(i, j), at(i, j + 1)), (at(i, j + 1), at(i, j))])
    return pairs


def solution(mesh):
    axes = ("gx", "gy")
    n_gx, n_gy = mesh.shape["gx"], mesh.shape["gy"]
    total = n_gx * n_gy
    pairs = swaps((n_gx, n_gy))

    def exchange(rows):
        return lax.all_to_all(rows, axes, 0, 0, tiled=True)

    def shards(
        right_side, pressure_head, vg_alpha, live_counts, partners,
        element_blocks, face_blocks, local_inverse, coarse_basis, coarse_inverse,
    ):
        alpha = vg_alpha.reshape(1, SLOTS)
        partial = pltpu.VMEM((8 * ROWS, SLOTS), F32)
        picked = pltpu.VMEM((3, NODES, SLOTS), F32)
        modal = pltpu.VMEM((MODES, SLOTS), F32)

        in_hbm = lambda x: pltpu.with_memory_space_constraint(x, pltpu.HBM)
        held = lambda x: jax.ShapeDtypeStruct(x.shape, x.dtype)
        semaphore = pltpu.SemaphoreType.DMA
        rows, b, mask, local_b, basis, local, inverse = call(
            restrict_kernel, "restrict", [pl.BlockSpec(memory_space=pltpu.SMEM)] + [HB] * 4,
            (vec(total, SLOTS), held(right_side), vec(8, SLOTS), vec(NODES, SLOTS), held(coarse_basis), held(local_inverse), held(coarse_inverse)),
            [partial, partial, semaphore, semaphore((PIECES,)), semaphore, semaphore],
        )(live_counts, *(in_hbm(x) for x in (right_side, coarse_basis, local_inverse, coarse_inverse)))
        gathered = exchange(rows)
        z1 = call(
            first_kernel, "first", [VM] * 5, vec(NODES, SLOTS), [pltpu.VMEM((SLOTS, SLOTS), F32), modal]
        )(mask, local_b, gathered, inverse, basis)

        def neighbours(z):
            return [lax.ppermute(z, axes, pairs[q]) for q in EARLY + LATER]

        def own(z, sources):
            return call(own_kernel, "own", [VM] * (6 + len(EARLY)), vec(NODES, SLOTS), [picked, partial])(
                z, element_blocks, pressure_head, alpha, partners, *sources, face_blocks
            )

        sources = neighbours(z1)
        w1, rows = call(
            image_kernel, "image", [VM] * (6 + len(LATER)),
            (vec(NODES, SLOTS), vec(total, SLOTS)), [picked, partial],
        )(own(z1, sources[: len(EARLY)]), mask, partners, *sources[len(EARLY) :], face_blocks, b, basis)
        gathered = exchange(rows)
        z2, v2, sums = call(
            second_kernel, "second", [VM] * 8,
            (vec(NODES, SLOTS), vec(NODES, SLOTS), vec(8, SLOTS)),
            [pltpu.VMEM((SLOTS, SLOTS), F32), partial, modal],
        )(b, w1, mask, z1, gathered, inverse, local, basis)
        sources = neighbours(z2)
        rows = call(
            last_image_kernel, "last_image", [VM] * (6 + len(LATER)),
            vec(total, SLOTS), [picked, partial],
        )(own(z2, sources[: len(EARLY)]), mask, partners, *sources[len(EARLY) :], face_blocks, b, v2)
        gathered = exchange(rows)
        update, hess = call(
            final_kernel, "final", [VM] * 4, (vec(NODES, SLOTS), vec(2, 3)), []
        )(sums, gathered, z1, z2)
        return update, hess.T

    placed = (
        P(None, axes), P(None, axes), P(axes), P(axes), P(None, axes),
        P(None, None, axes), P(None, None, None, axes), P(None, None, axes), P(None, None, axes),
        P(axes, None),
    )
    return jax.shard_map(
        shards, mesh=mesh, in_specs=placed, out_specs=(P(None, axes), P()), check_vma=False
    )
```

```python
import jax
import jax.numpy as jnp
from jax import lax
from jax.experimental import pallas as pl
from jax.experimental.pallas import tpu as pltpu
from jax.sharding import PartitionSpec as P

shape_exponent = 1.6
time_factor = 4.0
expo_m = 1.0 - 1.0 / shape_exponent

NODES = 64
MODES = 64
SLOTS = 128
DOTS = 8
ROWS = MODES + DOTS
F32 = jnp.float32
VM = pl.BlockSpec(memory_space=pltpu.VMEM)
HB = pl.BlockSpec(memory_space=pltpu.HBM)
PIECES = 4
UNROLL = 16
EARLY = (2, 1, 0)
LATER = (3,)


def live_mask(count):
    slots = lax.broadcasted_iota(jnp.int32, (8, SLOTS), 1)
    return (slots < count).astype(F32)


def tile_sum(block):
    parts = [block[8 * t : 8 * t + 8] for t in range(8)]
    while len(parts) > 1:
        parts = [a + b for a, b in zip(parts[::2], parts[1::2])]
    return parts[0]


def fold_rows(partial_ref, rows):
    parts = [partial_ref[pl.ds(k, rows, stride=8), :] for k in range(8)]
    while len(parts) > 1:
        parts = [a + b for a, b in zip(parts[::2], parts[1::2])]
    return parts[0]


def blocks_into(partial_ref, terms, first=0, last=NODES):
    def body(i, carry):
        total = None
        for block_at, vector in terms:
            part = tile_sum(block_at(i).astype(F32) * vector())
            total = part if total is None else total + part
        partial_ref[pl.ds(pl.multiple_of(8 * i, 8), 8), :] = total
        return carry

    lax.fori_loop(first, last, body, 0, unroll=UNROLL)


def send_row(partial_ref, out_ref):
    square = jnp.concatenate(
        [fold_rows(partial_ref, ROWS), jnp.zeros((SLOTS - ROWS, SLOTS), F32)], axis=0
    )
    row = jnp.sum(square.T, axis=0, keepdims=True)
    out_ref[...] = jnp.broadcast_to(row, out_ref.shape)


def put_dots(partial_ref, pairs):
    for k in range(DOTS):
        rows = pl.ds(8 * (MODES + k), 8)
        if k < len(pairs):
            left, right = pairs[k]
            partial_ref[rows, :] = tile_sum(left * right)
        else:
            partial_ref[rows, :] = jnp.zeros((8, SLOTS), F32)


def apply_local(local_ref, v_ref, partial_ref):
    blocks_into(partial_ref, [(lambda i: local_ref[i], lambda: v_ref[...])])
    return fold_rows(partial_ref, NODES)


def send_dots(pairs, out_ref):
    lane = lax.broadcasted_iota(jnp.int32, (1, SLOTS), 1)
    row = jnp.zeros((1, SLOTS), F32)
    for k, (left, right) in enumerate(pairs):
        total = jnp.sum(jnp.sum(tile_sum(left * right), axis=0, keepdims=True), axis=1, keepdims=True)
        row = jnp.where(lane == MODES + k, total, row)
    out_ref[...] = jnp.broadcast_to(row, out_ref.shape)


def restrict_kernel(
    count_ref, rhs_hbm, basis_hbm, local_hbm, inverse_hbm,
    row_ref, b_ref, mask_ref, local_b_ref, basis_ref, local_ref, inverse_ref,
    partial_ref, other_ref, rhs_sem, basis_sem, local_sem, inverse_sem,
):
    rhs_copy = pltpu.make_async_copy(rhs_hbm, b_ref, rhs_sem)
    rhs_copy.start()
    modes = MODES // PIECES
    copies = []
    for k in range(PIECES):
        piece = pl.ds(k * modes, modes)
        copies.append(pltpu.make_async_copy(basis_hbm.at[piece], basis_ref.at[piece], basis_sem.at[k]))
        copies[-1].start()
    local_copy = pltpu.make_async_copy(local_hbm, local_ref, local_sem)
    local_copy.start()
    inverse_copy = pltpu.make_async_copy(inverse_hbm, inverse_ref, inverse_sem)
    inverse_copy.start()
    put_dots(partial_ref, [])
    mask_ref[...] = live_mask(count_ref[0])
    rhs_copy.wait()
    b_ref[...] = b_ref[...] * mask_ref[0:1, :]
    for k, copy in enumerate(copies):
        copy.wait()
        blocks_into(
            partial_ref, [(lambda m: basis_ref[m], lambda: b_ref[...])], k * modes, (k + 1) * modes
        )
    send_row(partial_ref, row_ref)
    local_copy.wait()
    local_b_ref[...] = apply_local(local_ref, b_ref, other_ref)
    inverse_copy.wait()


def halves(rows_ref):
    lane = lax.broadcasted_iota(jnp.int32, (SLOTS, SLOTS), 1)
    even = rows_ref[pl.ds(0, SLOTS, stride=2), :]
    odd = rows_ref[pl.ds(1, SLOTS, stride=2), :]
    return jnp.where(lane < MODES, even, pltpu.roll(odd, MODES, 1))


def coarse_part(start, coarse_ref, inverse_ref, basis_ref, modal_ref):
    def coarse_step(t, acc):
        column = inverse_ref[:, pl.ds(pl.multiple_of(t * SLOTS, SLOTS), SLOTS)].astype(F32)
        return acc + column * coarse_ref[pl.ds(t, 1), :]

    acc = lax.fori_loop(0, 2 * MODES, coarse_step, jnp.zeros((MODES, SLOTS), F32), unroll=2 * UNROLL)
    modal_ref[...] = jnp.broadcast_to(jnp.sum(acc, axis=1, keepdims=True), (MODES, SLOTS))

    def prolong_step(m, total):
        return total + basis_ref[m].astype(F32) * modal_ref[pl.ds(m, 1), :]

    return lax.fori_loop(0, MODES, prolong_step, start, unroll=2 * UNROLL)


def first_kernel(
    mask_ref, local_b_ref, gathered_ref, inverse_ref, basis_ref, z_ref, coarse_ref, modal_ref
):
    coarse_ref[...] = halves(gathered_ref)
    z = coarse_part(local_b_ref[...], coarse_ref, inverse_ref, basis_ref, modal_ref)
    z_ref[...] = z * mask_ref[0:1, :]


def lane_of(row, k):
    lane = lax.broadcasted_iota(jnp.int32, row.shape, 1)
    return jnp.sum(jnp.where(lane == k, row, 0.0), axis=1, keepdims=True)


def second_kernel(
    b_ref, w_ref, mask_ref, z1_ref, gathered_ref, inverse_ref, local_ref, basis_ref,
    z_ref, v_ref, sums_ref, coarse_ref, partial_ref, modal_ref,
):
    sums = jnp.sum(gathered_ref[...], axis=0, keepdims=True)
    sums_ref[...] = jnp.broadcast_to(sums, sums_ref.shape)
    along = lane_of(sums, MODES) / lane_of(sums, MODES + 2)
    scale = 1.0 / jnp.sqrt(lane_of(sums, MODES + 1))
    v_ref[...] = (w_ref[...] - along * b_ref[...]) * scale
    coarse_ref[...] = halves(gathered_ref)
    local_part = apply_local(local_ref, w_ref, partial_ref)
    z = coarse_part(local_part, coarse_ref, inverse_ref, basis_ref, modal_ref)
    z_ref[...] = (z * mask_ref[0:1, :] - along * z1_ref[...]) * scale


def face_of(q):
    if q < 2:
        odd = lax.rem(lax.axis_index("gx"), 2)
        return 1 - odd if q == 0 else odd
    odd = lax.rem(lax.axis_index("gy"), 2)
    return 3 - odd if q == 2 else 2 + odd


def pick(source_ref, partners_ref, q):
    slots = jnp.broadcast_to(partners_ref[pl.ds(face_of(q), 1), :], (NODES, SLOTS))
    return jnp.take_along_axis(source_ref[...], slots, axis=1)


def face_terms(qs, source_refs, partners_ref, faces_ref, picked_ref):
    terms = []
    for k, (q, source_ref) in enumerate(zip(qs, source_refs)):
        picked_ref[k] = pick(source_ref, partners_ref, q)
        face = face_of(q)
        terms.append((lambda i, face=face: faces_ref[face, i], lambda k=k: picked_ref[k]))
    return terms


def own_kernel(z_ref, blocks_ref, pressure_ref, alpha_ref, partners_ref, *refs):
    source_refs, (faces_ref, out_ref, picked_ref, partial_ref) = refs[: len(EARLY)], refs[len(EARLY) :]
    terms = face_terms(EARLY, source_refs, partners_ref, faces_ref, picked_ref)
    blocks_into(partial_ref, [(lambda i: blocks_ref[i], lambda: z_ref[...])] + terms)
    alpha = alpha_ref[...]
    scaled = jnp.abs(alpha * pressure_ref[...])
    power = jnp.exp((shape_exponent - 1.0) * jnp.log(scaled))
    tail = jnp.exp(-(expo_m + 1.0) * jnp.log(1.0 + power * scaled))
    storage = (time_factor * shape_exponent * expo_m) * alpha * power * tail
    out_ref[...] = fold_rows(partial_ref, NODES) + storage * z_ref[...]


def all_blocks(own_ref, mask_ref, partners_ref, source_refs, faces_ref, picked_ref, partial_ref):
    blocks_into(partial_ref, face_terms(LATER, source_refs, partners_ref, faces_ref, picked_ref))
    return (own_ref[...] + fold_rows(partial_ref, NODES)) * mask_ref[0:1, :]


def image_kernel(own_ref, mask_ref, partners_ref, *refs):
    source_refs, refs = refs[: len(LATER)], refs[len(LATER) :]
    blocks_ref, b_ref, basis_ref, w_ref, row_ref, picked_ref, partial_ref = refs
    w_ref[...] = all_blocks(own_ref, mask_ref, partners_ref, source_refs, blocks_ref, picked_ref, partial_ref)
    blocks_into(partial_ref, [(lambda m: basis_ref[m], lambda: w_ref[...])])
    w = w_ref[...]
    b = b_ref[...]
    put_dots(partial_ref, [(w, b), (w, w), (b, b)])
    send_row(partial_ref, row_ref)


def last_image_kernel(own_ref, mask_ref, partners_ref, *refs):
    source_refs, refs = refs[: len(LATER)], refs[len(LATER) :]
    blocks_ref, b_ref, v_ref, row_ref, picked_ref, partial_ref = refs
    w = all_blocks(own_ref, mask_ref, partners_ref, source_refs, blocks_ref, picked_ref, partial_ref)
    b = b_ref[...]
    v = v_ref[...]
    send_dots([(w, b), (w, v), (w, w), (v, v), (b, v)], row_ref)


def final_kernel(first_ref, gathered_ref, z1_ref, z2_ref, update_ref, hess_ref):
    sums = first_ref[0:1, :]
    late = jnp.sum(gathered_ref[...], axis=0, keepdims=True)
    wb, ww, bb = (lane_of(sums, MODES + k) for k in range(3))
    xb, xv, xx, vv, bv = (lane_of(late, MODES + k) for k in range(5))
    beta = jnp.sqrt(bb)
    size = jnp.sqrt(vv)
    h11 = wb / bb
    h21 = size * jnp.sqrt(ww) / beta
    h12 = xb / (size * beta)
    h22 = xv / vv
    cross = bv / (beta * size)
    rest = xx / vv - h12 * h12 - h22 * h22 + 2.0 * h12 * h22 * cross
    h32 = jnp.sqrt(jnp.maximum(rest, 0.0))
    gram_aa = h11 * h11 + h21 * h21
    gram_ab = h11 * h12 + h21 * h22
    gram_bb = h12 * h12 + h22 * h22 + h32 * h32
    target_a = beta * h11
    target_b = beta * h12
    determinant = gram_aa * gram_bb - gram_ab * gram_ab
    weight_one = (gram_bb * target_a - gram_ab * target_b) / determinant
    weight_two = (gram_aa * target_b - gram_ab * target_a) / determinant
    update_ref[...] = (weight_one / beta) * z1_ref[...] + (weight_two / size) * z2_ref[...]
    row = lax.broadcasted_iota(jnp.int32, (2, 3), 0)
    col = lax.broadcasted_iota(jnp.int32, (2, 3), 1)
    hess = jnp.where(row == 0, jnp.where(col == 0, h11, h21), jnp.where(col == 0, h12, jnp.where(col == 1, h22, h32)))
    hess_ref[...] = jnp.where((row == 0) & (col == 2), 0.0, hess)


def vec(*shape):
    return jax.ShapeDtypeStruct(shape, F32)


def call(body, name, specs, outs, scratch, megabytes=4):
    return pl.pallas_call(
        body,
        name=name,
        in_specs=specs,
        out_specs=jax.tree.map(lambda _: VM, outs),
        out_shape=outs,
        scratch_shapes=scratch,
        compiler_params=pltpu.CompilerParams(vmem_limit_bytes=megabytes << 20),
    )


def swaps(mesh_shape):
    n_gx, n_gy = mesh_shape
    at = lambda i, j: i * n_gy + j
    pairs = ([], [], [], [])
    for i in range(n_gx):
        for j in range(n_gy):
            if i + 1 < n_gx:
                pairs[i % 2].extend([(at(i, j), at(i + 1, j)), (at(i + 1, j), at(i, j))])
            if j + 1 < n_gy:
                pairs[2 + j % 2].extend([(at(i, j), at(i, j + 1)), (at(i, j + 1), at(i, j))])
    return pairs


def solution(mesh):
    axes = ("gx", "gy")
    n_gx, n_gy = mesh.shape["gx"], mesh.shape["gy"]
    total = n_gx * n_gy
    pairs = swaps((n_gx, n_gy))

    def exchange(rows):
        return lax.all_to_all(rows, axes, 0, 0, tiled=True)

    def shards(
        right_side, pressure_head, vg_alpha, live_counts, partners,
        element_blocks, face_blocks, local_inverse, coarse_basis, coarse_inverse,
    ):
        alpha = vg_alpha.reshape(1, SLOTS)
        partial = pltpu.VMEM((8 * ROWS, SLOTS), F32)
        picked = pltpu.VMEM((3, NODES, SLOTS), F32)
        modal = pltpu.VMEM((MODES, SLOTS), F32)

        in_hbm = lambda x: pltpu.with_memory_space_constraint(x, pltpu.HBM)
        held = lambda x: jax.ShapeDtypeStruct(x.shape, x.dtype)
        semaphore = pltpu.SemaphoreType.DMA
        rows, b, mask, local_b, basis, local, inverse = call(
            restrict_kernel, "restrict", [pl.BlockSpec(memory_space=pltpu.SMEM)] + [HB] * 4,
            (vec(total, SLOTS), held(right_side), vec(8, SLOTS), vec(NODES, SLOTS), held(coarse_basis), held(local_inverse), held(coarse_inverse)),
            [partial, partial, semaphore, semaphore((PIECES,)), semaphore, semaphore],
        )(live_counts, *(in_hbm(x) for x in (right_side, coarse_basis, local_inverse, coarse_inverse)))
        gathered = exchange(rows)
        z1 = call(
            first_kernel, "first", [VM] * 5, vec(NODES, SLOTS), [pltpu.VMEM((SLOTS, SLOTS), F32), modal]
        )(mask, local_b, gathered, inverse, basis)

        def neighbours(z):
            return [lax.ppermute(z, axes, pairs[q]) for q in EARLY + LATER]

        def own(z, sources):
            return call(own_kernel, "own", [VM] * (6 + len(EARLY)), vec(NODES, SLOTS), [picked, partial])(
                z, element_blocks, pressure_head, alpha, partners, *sources, face_blocks
            )

        sources = neighbours(z1)
        w1, rows = call(
            image_kernel, "image", [VM] * (6 + len(LATER)),
            (vec(NODES, SLOTS), vec(total, SLOTS)), [picked, partial],
        )(own(z1, sources[: len(EARLY)]), mask, partners, *sources[len(EARLY) :], face_blocks, b, basis)
        gathered = exchange(rows)
        z2, v2, sums = call(
            second_kernel, "second", [VM] * 8,
            (vec(NODES, SLOTS), vec(NODES, SLOTS), vec(8, SLOTS)),
            [pltpu.VMEM((SLOTS, SLOTS), F32), partial, modal],
        )(b, w1, mask, z1, gathered, inverse, local, basis)
        sources = neighbours(z2)
        rows = call(
            last_image_kernel, "last_image", [VM] * (6 + len(LATER)),
            vec(total, SLOTS), [picked, partial],
        )(own(z2, sources[: len(EARLY)]), mask, partners, *sources[len(EARLY) :], face_blocks, b, v2)
        gathered = exchange(rows)
        update, hess = call(
            final_kernel, "final", [VM] * 4, (vec(NODES, SLOTS), vec(2, 3)), []
        )(sums, gathered, z1, z2)
        return update, hess.T

    placed = (
        P(None, axes), P(None, axes), P(axes), P(axes), P(None, axes),
        P(None, None, axes), P(None, None, None, axes), P(None, None, axes), P(None, None, axes),
        P(axes, None),
    )
    return jax.shard_map(
        shards, mesh=mesh, in_specs=placed, out_specs=(P(None, axes), P()), check_vma=False
    )
```
